32 devices in a mesh: dp: 32 (over z, y, x, core).
Axes of the slice: x: 2, y: 2, z: 4, core: 2. Of those that a mesh axis runs over, the one named last changes fastest.
Arguments:
- block_input: bfloat16 [640, 197, 384], P('dp'), may hold values from -6 to 6
- first_gain: float32 [384], replicated, may hold values from 0.5 to 1.5
- first_shift: float32 [384], replicated, may hold values from -3 to 3
- qkv_weight: bfloat16 [384, 1152], P('dp'), may hold values from -0.3125 to 0.3125
- query_value_bias: float32 [768], replicated, may hold values from -3 to 3
- proj_weight: bfloat16 [384, 384], P('dp'), may hold values from -1.25 to 1.25
- proj_bias: float32 [384], replicated, may hold values from -3 to 3
- second_gain: float32 [384], replicated, may hold values from 0.5 to 1.5
- second_shift: float32 [384], replicated, may hold values from -3 to 3
- up_weight: bfloat16 [384, 1536], P('dp'), may hold values from -0.3125 to 0.3125
- up_bias: float32 [1536], replicated, may hold values from -3 to 3
- down_weight: bfloat16 [1536, 384], P('dp'), may hold values from -0.15625 to 0.15625
- down_bias: float32 [384], replicated, may hold values from -3 to 3
- output_cotangent: bfloat16 [640, 197, 384], P('dp'), may hold values from -6 to 6
Outputs:
- block_output: float32 [640, 197, 384], P('dp')
- input_grad: float32 [640, 197, 384], P('dp')
- grad_first_gain: float32 [384], P('dp')
- grad_first_shift: float32 [384], P('dp')
- grad_qkv_weight: float32 [384, 1152], P('dp')
- grad_query_value_bias: float32 [768], P('dp')
- grad_proj_weight: float32 [384, 384], P('dp')
- grad_proj_bias: float32 [384], P('dp')
- grad_second_gain: float32 [384], P('dp')
- grad_second_shift: float32 [384], P('dp')
- grad_up_weight: float32 [384, 1536], P('dp')
- grad_up_bias: float32 [1536], P('dp')
- grad_down_weight: float32 [1536, 384], P('dp')
- grad_down_bias: float32 [384], P('dp')
The draws below stay inside these ranges and needn't reach their ends.
All inputs are finite; a program needn't handle non-finite values.
Results may differ from the reference program's by a relative error of at most 0.011.
Values may be sent and summed in bfloat16 or wider, within the bound.
No kernel may reach another device: no remote copies, remote signals or barrier semaphores. Data moves between devices by JAX's collectives and lax.ppermute only.
A program may use at most 256 MiB of HBM per device.

```python
import jax
import jax.numpy as jnp
from jax import lax

D = 384
H = 6
DH = 64
FF = 1536
S = 197
IMAGES = 640


def steps_of(key, extent, pieces, least, largest):
    def one(position, parts):
        heights = jax.random.uniform(jax.random.fold_in(jax.random.fold_in(key, 6), position), (parts,), jnp.float32, least / len(pieces), largest / len(pieces))
        return jnp.repeat(jnp.exp(heights), extent[position] // parts).reshape((-1,) + (1,) * (len(extent) - position - 1))

    factor_of = one(*pieces[0])
    for cut in pieces[1:]:
        factor_of = factor_of * one(*cut)
    return factor_of


def noise(stream_key, dims, width, most, split=(), kind=jnp.bfloat16):
    factor_of = steps_of(stream_key, dims, split, -0.22, 0.18) if split else 1.0
    drawn = jax.random.normal(stream_key, dims, jnp.float32) * width * factor_of
    return jnp.minimum(jnp.maximum(drawn, -most), most).astype(kind)


def setup_inputs(seed: int = 0) -> dict:
    key_of = jax.random.split(jax.random.key(seed), 15)
    block_input = noise(key_of[0], (IMAGES, S, D), 1.0, 6.0, ((0, 32),))
    first_gain = jnp.clip(1.0 + 0.1 * jax.random.normal(key_of[1], (D,), jnp.float32), 0.5, 1.5)
    first_shift = noise(key_of[2], (D,), 0.5, 3.0, (), jnp.float32)
    qkv_weight = noise(key_of[3], (D, 3 * D), D ** -0.5, 0.3125, ((0, 32),))
    query_value_bias = noise(key_of[4], (2 * D,), 0.5, 3.0, (), jnp.float32)
    proj_weight = noise(key_of[5], (D, D), (D // 16) ** -0.5, 1.25, ((0, 32),))
    proj_bias = noise(key_of[6], (D,), 0.5, 3.0, (), jnp.float32)
    second_gain = jnp.clip(1.0 + 0.1 * jax.random.normal(key_of[7], (D,), jnp.float32), 0.5, 1.5)
    second_shift = noise(key_of[8], (D,), 0.5, 3.0, (), jnp.float32)
    up_weight = noise(key_of[9], (D, FF), D ** -0.5, 0.3125, ((0, 32),))
    up_bias = noise(key_of[10], (FF,), 0.5, 3.0, (), jnp.float32)
    down_weight = noise(key_of[11], (FF, D), FF ** -0.5, 0.15625, ((0, 32),))
    down_bias = noise(key_of[12], (D,), 0.5, 3.0, (), jnp.float32)
    output_cotangent = noise(key_of[13], (IMAGES, S, D), 1.0, 6.0, ((0, 32),))
    return dict(block_input=block_input, first_gain=first_gain, first_shift=first_shift, qkv_weight=qkv_weight, query_value_bias=query_value_bias, proj_weight=proj_weight, proj_bias=proj_bias, second_gain=second_gain, second_shift=second_shift, up_weight=up_weight, up_bias=up_bias, down_weight=down_weight, down_bias=down_bias, output_cotangent=output_cotangent)


@jax.custom_vjp
def low(v):
    return lax.optimization_barrier(v.astype(jnp.bfloat16)).astype(jnp.float32)

@jax.custom_vjp
def low_back(v):
    return v

def low_keep(v):
    return (low(v), None)

def low_pass(kept, grad):
    return (grad,)

def back_keep(v):
    return (v, None)

def back_low(kept, grad):
    return (low(grad),)
low.defvjp(low_keep, low_pass)
low_back.defvjp(back_keep, back_low)
highest = lax.Precision.HIGHEST
norm_eps = 1e-06

def layer_norm(values, gain, shift):
    center = values - lax.optimization_barrier(jnp.mean(values, axis=-1, keepdims=True))
    spread = lax.optimization_barrier(jnp.mean(center * center, axis=-1, keepdims=True))
    return center * lax.rsqrt(spread + norm_eps) * gain + shift

def forward(block_input, first_gain, first_shift, qkv_weight, query_value_bias, proj_weight, proj_bias, second_gain, second_shift, up_weight, up_bias, down_weight, down_bias):
    count = block_input.shape[0]
    normed = low(layer_norm(block_input, first_gain, first_shift))
    full_bias = jnp.concatenate([query_value_bias[:D], jnp.zeros((D,), jnp.float32), query_value_bias[D:]])
    packed = jnp.einsum('isd,de->ise', normed, qkv_weight, precision=highest) + full_bias
    packed = low(low_back(packed))
    query_rows = packed[..., :D].reshape(count, S, H, DH)
    key_rows = packed[..., D:2 * D].reshape(count, S, H, DH)
    value_rows = packed[..., 2 * D:].reshape(count, S, H, DH)
    scores = low_back(jnp.einsum('iqhe,ikhe->ihqk', query_rows, key_rows, precision=highest) * 0.125)
    weights = low(jax.nn.softmax(scores, axis=-1))
    mixed = jnp.einsum('ihqk,ikhe->iqhe', weights, value_rows, precision=highest).reshape(count, S, D)
    mixed = low(low_back(mixed))
    branch = low_back(jnp.einsum('isd,de->ise', mixed, proj_weight, precision=highest) + proj_bias)
    middle = block_input + branch
    second = low(layer_norm(middle, second_gain, second_shift))
    upper = low_back(jnp.einsum('isd,df->isf', second, up_weight, precision=highest) + up_bias)
    hidden = low(jax.nn.gelu(upper, approximate=False))
    lower = low_back(jnp.einsum('isf,fd->isd', hidden, down_weight, precision=highest) + down_bias)
    return middle + lower

def reference(block_input, first_gain, first_shift, qkv_weight, query_value_bias, proj_weight, proj_bias, second_gain, second_shift, up_weight, up_bias, down_weight, down_bias, output_cotangent):
    params = (block_input, first_gain, first_shift, qkv_weight, query_value_bias, proj_weight, proj_bias, second_gain, second_shift, up_weight, up_bias, down_weight, down_bias)
    params = tuple((p.astype(jnp.float32) for p in params))
    output, pullback = jax.vjp(forward, *params)
    grads = pullback(output_cotangent.astype(jnp.float32))
    return (output, grads[0], grads[1], grads[2], grads[3], grads[4], grads[5], grads[6], grads[7], grads[8], grads[9], grads[10], grads[11], grads[12])
```

```python
import jax
import jax.numpy as jnp
from jax import lax
from jax.experimental import pallas as pl
from jax.experimental.pallas import tpu as pltpu
from jax.sharding import PartitionSpec as P

D = 384
H = 6
DH = 64
FF = 1536
S = 197
SR = 208
SL = 256
CH = 256
norm_eps = 1e-06
f32 = jnp.float32
bf16 = jnp.bfloat16
NN = (((1,), (0,)), ((), ()))
NT = (((1,), (1,)), ((), ()))
TN = (((0,), (0,)), ((), ()))


def dot(a, b, dims):
    return lax.dot_general(a, b, dims, preferred_element_type=f32)


def norm(x):
    c = x - jnp.mean(x, axis=-1, keepdims=True)
    r = lax.rsqrt(jnp.mean(c * c, axis=-1, keepdims=True) + norm_eps)
    return c * r, r


def for_parity(me, body):
    for parity in (0, 1):
        @pl.when((me & 1) == parity)
        def _():
            body(parity)


def attn_fwd(me_ref, ga_ref, gb_ref, x_ref, g_ref, b_ref, bias_ref,
             pt_ref, wt_ref, ot_ref, w_ref, a_s, wT_s, *, n):
    me = me_ref[0]
    rows_of = D // n

    @pl.when(pl.program_id(0) == 0)
    def _():
        a_s[...] = jnp.zeros_like(a_s)

        def gather(parity):
            for k in range(n):
                src = ga_ref if (k & 1) == parity else gb_ref
                w_ref[rows_of * k : rows_of * (k + 1), :] = src[(me ^ k) >> 1]

        for_parity(me, gather)
        wT_s[...] = w_ref[...].T

    n1, _ = norm(x_ref[0].astype(f32))
    a_s[:S, :] = (n1 * g_ref[...] + b_ref[...]).astype(bf16)
    for j in range(9):
        rows = slice(128 * j, 128 * (j + 1))
        pT = dot(wT_s[rows, :], a_s[...], NT) + bias_ref[rows, :]
        pt_ref[0, rows, :] = pT.astype(bf16)
    scale = 0.125 * 1.4426950408889634
    valid = lax.broadcasted_iota(jnp.int32, (16, SL), 0) < S - 192
    for h in range(H):
        qT = pt_ref[0, 64 * h : 64 * h + 64, :]
        kT = pt_ref[0, D + 64 * h : D + 64 * h + 64, :SR]
        vT = pt_ref[0, 2 * D + 64 * h : 2 * D + 64 * h + 64, :SR]
        z = dot(kT, qT, TN)
        zt = z[:192]
        zb = jnp.where(valid, z[192:], -jnp.inf)
        m = jnp.maximum(jnp.max(zt, axis=0, keepdims=True), jnp.max(zb, axis=0, keepdims=True))
        et = jnp.exp2((zt - m) * scale)
        eb = jnp.exp2((zb - m) * scale)
        l = jnp.sum(et, axis=0, keepdims=True) + jnp.sum(eb, axis=0, keepdims=True)
        inv = 1.0 / l
        wt_ref[0, h, :192, :] = (et * inv).astype(bf16)
        wt_ref[0, h, 192:, :] = (eb * inv).astype(bf16)
        ot_ref[0, 64 * h : 64 * h + 64, :] = dot(vT, wt_ref[0, h], NN).astype(bf16)


ERF_P = 0.3275911
ERF_A = (0.254829592, -0.284496736, 1.421413741, -1.453152027, 1.061405429)


def gelu_parts(u):
    e = jnp.exp2(u * u * (-0.5 * 1.4426950408889634))
    t = 1.0 / (1.0 + jnp.abs(u) * (ERF_P * 0.7071067811865476))
    poly = ERF_A[4] * 0.5
    for a in ERF_A[3::-1]:
        poly = poly * t + a * 0.5
    q = poly * t * e
    phi = jnp.where(u >= 0, 1.0 - q, q)
    return u * phi, phi + u * (e * 0.3989422804014327)


def spread(vec, width, shift, n):
    size = n * width
    d = lax.broadcasted_iota(jnp.int32, (n, size), 1)
    k = lax.broadcasted_iota(jnp.int32, (n, size), 0)
    picked = jnp.where(d // width == k, jnp.broadcast_to(vec, (n, size)), 0.0).astype(bf16)
    dd = lax.broadcasted_iota(jnp.int32, (size, 128), 0)
    j = lax.broadcasted_iota(jnp.int32, (size, 128), 1)
    place = jnp.where(dd % width + shift == j, 1.0, 0.0).astype(bf16)
    return dot(picked, place, NN)


def emit(me, stage, keep_ref, send_ref, n, bits):
    def one(k, carry):
        m = me ^ k
        pos = 0
        for b in bits:
            pos = pos * 2 + ((m >> b) & 1)

        @pl.when((m & 1) == 0)
        def _():
            keep_ref[pos] = stage[k]

        @pl.when((m & 1) == 1)
        def _():
            send_ref[pos] = stage[k].astype(bf16)
        return carry

    lax.fori_loop(0, n, one, 0)


def mlp(me_ref, ga_ref, gb_ref, x_ref, ot_ref, e_ref, pb_ref, g_ref, b_ref, ub_ref, db_ref,
        out_ref, dx1_ref, dot_ref, keep_ref, send_ref,
        xs, es, fs, pj_s, up_s, dn_s, gup, gdn, gpj, small, stage, *, n, bits):
    me = me_ref[0]
    step = pl.program_id(0)
    r1, r4 = D // n, FF // n

    @pl.when(step == 0)
    def _():
        xs[...] = jnp.zeros_like(xs)
        es[...] = jnp.zeros_like(es)
        fs[...] = jnp.zeros_like(fs)
        gup[...] = jnp.zeros_like(gup)
        gdn[...] = jnp.zeros_like(gdn)
        gpj[...] = jnp.zeros_like(gpj)
        small[...] = jnp.zeros_like(small)

        def gather(parity):
            for k in range(n):
                src = ga_ref if (k & 1) == parity else gb_ref
                part = src[(me ^ k) >> 1]
                rows = slice(r1 * k, r1 * (k + 1))
                pj_s[rows, :] = part[:r1]
                for q in range(4):
                    up_s[rows, D * q : D * (q + 1)] = part[r1 * (1 + q) : r1 * (2 + q)]
                dn_s[r4 * k : r4 * (k + 1), :] = part[5 * r1 :]

        for_parity(me, gather)

    xs[:S, :] = x_ref[0]
    es[:S, :] = e_ref[0]
    oT = ot_ref[0, :, :SR]
    x1 = xs[...].astype(f32) + dot(oT, pj_s[...], TN) + pb_ref[...]
    n2, r2 = norm(x1)
    bb = (n2 * g_ref[...] + b_ref[...]).astype(bf16)
    bT = bb.T
    e2 = es[...]
    eT = e2.T
    acc = x1 + db_ref[...]
    dB = jnp.zeros((SR, D), f32)

    def fold(v):
        return jnp.sum(v.reshape(SR // 8, 8, v.shape[1]), axis=0)

    for c in range(FF // CH):
        cols = slice(c * CH, (c + 1) * CH)
        u = dot(bb, up_s[:, cols], NN) + ub_ref[:, cols]
        g, gp = gelu_parts(u)
        gb = g.astype(bf16)
        acc = acc + dot(gb, dn_s[cols, :], NN)
        dU = (dot(e2, dn_s[cols, :], NT) * gp).astype(bf16)
        small[:, FF + c * CH : FF + (c + 1) * CH] += fold(dU.astype(f32))
        dB = dB + dot(dU, up_s[:, cols], NT)
        gdn[:, cols] += dot(eT, gb, NN)
        gup[:, cols] += dot(bT, dU, NN)
    out_ref[0] = acc[:S]
    dn = dB * g_ref[...]
    ef = e2.astype(f32)
    dx1 = ef + r2 * (dn - jnp.mean(dn, axis=-1, keepdims=True) - n2 * jnp.mean(dn * n2, axis=-1, keepdims=True))
    dx1_ref[0] = dx1[:S]
    ff = dx1.astype(bf16)
    fs[:SR, :] = ff
    small[:, 0:D] += fold(dB * n2)
    small[:, D : 2 * D] += fold(dB)
    small[:, 2 * D : 3 * D] += fold(ff.astype(f32))
    small[:, 3 * D : 4 * D] += fold(ef)
    gpj[...] += dot(oT, ff, NN)
    dot_ref[0] = dot(pj_s[...], fs[...], NT).astype(bf16)

    @pl.when(step == pl.num_programs(0) - 1)
    def _():
        tot = jnp.sum(small[...], axis=0, keepdims=True)
        sm = spread(tot[:, FF:], r4, 4 * r1, n)
        for q in range(4):
            sm = sm + spread(tot[:, D * q : D * (q + 1)], r1, r1 * q, n)
        for k in range(n):
            rows = slice(r1 * k, r1 * (k + 1))
            stage[k, :r1, :] = gpj[rows, :]
            for q in range(4):
                stage[k, r1 * (1 + q) : r1 * (2 + q), :] = gup[rows, D * q : D * (q + 1)]
            stage[k, 9 * r1 : 9 * r1 + 1, :128] = sm[k : k + 1]
        for c in range(FF // 384):
            gT = gdn[:, 384 * c : 384 * (c + 1)].T
            for k in range(384 // r4):
                stage[c * (384 // r4) + k, 5 * r1 : 9 * r1, :] = gT[r4 * k : r4 * (k + 1)]
        emit(me, stage, keep_ref, send_ref, n, bits)


def attn_bwd(me_ref, x_ref, pt_ref, wt_ref, dot_ref, dx1_ref, g_ref, b_ref, w_ref,
             din_ref, keep_ref, send_ref, as_, dp_s, gq, small, stage, *, n, bits):
    me = me_ref[0]
    step = pl.program_id(0)
    r1 = D // n

    @pl.when(step == 0)
    def _():
        as_[:, :D] = jnp.zeros((SR, D), bf16)
        as_[:, D:] = jnp.ones((SR, 128), bf16)
        gq[...] = jnp.zeros_like(gq)
        small[...] = jnp.zeros_like(small)

    n1, rr = norm(x_ref[0].astype(f32))
    as_[:S, :D] = (n1 * g_ref[...] + b_ref[...]).astype(bf16)
    for h in range(H):
        hs = slice(64 * h, 64 * h + 64)
        ks = slice(D + 64 * h, D + 64 * h + 64)
        vs = slice(2 * D + 64 * h, 2 * D + 64 * h + 64)
        qT = pt_ref[0, hs, :]
        kT = pt_ref[0, ks, :SR]
        vT = pt_ref[0, vs, :SR]
        doT = dot_ref[0, hs, :]
        wt = wt_ref[0, h]
        w = wt.astype(f32)
        dW = dot(vT, doT, TN)
        t = dW * w
        dZ = (t - w * jnp.sum(t, axis=0, keepdims=True)).astype(bf16)
        dp_s[hs, :] = (dot(kT, dZ, NN) * 0.125)[:, :SR].astype(bf16)
        dp_s[ks, :] = (dot(qT, dZ, NT) * 0.125).astype(bf16)
        dp_s[vs, :] = dot(doT, wt, NT).astype(bf16)
    gq[...] += dot(dp_s[...], as_[...], NN)
    dA = dot(dp_s[...], w_ref[...], (((0,), (1,)), ((), ())))[:S]
    dm = dA * g_ref[...]
    din_ref[0] = dx1_ref[0] + rr * (
        dm - jnp.mean(dm, axis=-1, keepdims=True) - n1 * jnp.mean(dm * n1, axis=-1, keepdims=True))
    small[0:1, 0:D] += jnp.sum(dA * n1, axis=0, keepdims=True)
    small[0:1, D : 2 * D] += jnp.sum(dA, axis=0, keepdims=True)

    @pl.when(step == pl.num_programs(0) - 1)
    def _():
        cs = gq[:, D : D + 128].T[0:1, :]
        sm = spread(small[0:1, :D], r1, 0, n) + spread(small[0:1, D : 2 * D], r1, r1, n)
        sm = sm + spread(jnp.concatenate([cs[:, :D], cs[:, 2 * D :]], axis=1), 2 * r1, 2 * r1, n)
        for q in range(3):
            gT = gq[D * q : D * (q + 1), :D].T
            for k in range(n):
                stage[k, r1 * q : r1 * (q + 1), :] = gT[r1 * k : r1 * (k + 1)]
        for k in range(n):
            stage[k, 3 * r1 : 3 * r1 + 1, :128] = sm[k : k + 1]
        emit(me, stage, keep_ref, send_ref, n, bits)


def img(shape):
    return pl.BlockSpec((1,) + shape, lambda i: (i,) + (0,) * len(shape))


def res(shape):
    return pl.BlockSpec(shape, lambda i: (0,) * len(shape))


smem = pl.BlockSpec(memory_space=pltpu.SMEM)
params = pltpu.CompilerParams(dimension_semantics=("arbitrary",), vmem_limit_bytes=60 * 2**20)


def shape_of(*dims, dtype=f32):
    return jax.ShapeDtypeStruct(dims, dtype)


def run_fwd(n, me, ga, gb, x, g1, b1, bias):
    m = x.shape[0]
    return pl.pallas_call(
        lambda *refs: attn_fwd(*refs, n=n), grid=(m,), name="attn_fwd",
        in_specs=[smem, res(ga.shape), res(gb.shape), img((S, D)), res((1, D)), res((1, D)), res((3 * D, SL))],
        out_specs=[img((3 * D, SL)), img((H, SR, SL)), img((D, SL)), res((D, 3 * D))],
        out_shape=[shape_of(m, 3 * D, SL, dtype=bf16), shape_of(m, H, SR, SL, dtype=bf16),
                   shape_of(m, D, SL, dtype=bf16), shape_of(D, 3 * D, dtype=bf16)],
        scratch_shapes=[pltpu.VMEM((SL, D), bf16), pltpu.VMEM((3 * D, D), bf16)],
        compiler_params=params,
    )(me, ga, gb, x, g1, b1, bias)


def chunk_rows(n, parts):
    return -(-(parts * (D // n) + 1) // 16) * 16


def run_mlp(n, bits, me, ga, gb, x, oT, e, pb, g2, b2, ub, db):
    m = x.shape[0]
    cr = chunk_rows(n, 9)
    return pl.pallas_call(
        lambda *refs: mlp(*refs, n=n, bits=bits), grid=(m,), name="mlp",
        in_specs=[smem, res(ga.shape), res(gb.shape), img((S, D)), img((D, SL)), img((S, D)),
                  res((1, D)), res((1, D)), res((1, D)), res((1, FF)), res((1, D))],
        out_specs=[img((S, D)), img((S, D)), img((D, SL)), res((n // 2, cr, D)), res((n // 2, cr, D))],
        out_shape=[shape_of(m, S, D), shape_of(m, S, D), shape_of(m, D, SL, dtype=bf16),
                   shape_of(n // 2, cr, D), shape_of(n // 2, cr, D, dtype=bf16)],
        scratch_shapes=[pltpu.VMEM((SR, D), bf16), pltpu.VMEM((SR, D), bf16), pltpu.VMEM((SL, D), bf16),
                        pltpu.VMEM((D, D), bf16), pltpu.VMEM((D, FF), bf16), pltpu.VMEM((FF, D), bf16),
                        pltpu.VMEM((D, FF), f32), pltpu.VMEM((D, FF), f32), pltpu.VMEM((D, D), f32),
                        pltpu.VMEM((8, 2 * FF), f32), pltpu.VMEM((n, cr, D), f32)],
        compiler_params=params,
    )(me, ga, gb, x, oT, e, pb, g2, b2, ub, db)


def run_bwd(n, bits, me, x, pt, wt, doT, dx1, g1, b1, qkv):
    m = x.shape[0]
    cr = chunk_rows(n, 3)
    return pl.pallas_call(
        lambda *refs: attn_bwd(*refs, n=n, bits=bits), grid=(m,), name="attn_bwd",
        in_specs=[smem, img((S, D)), img((3 * D, SL)), img((H, SR, SL)), img((D, SL)), img((S, D)),
                  res((1, D)), res((1, D)), res((D, 3 * D))],
        out_specs=[img((S, D)), res((n // 2, cr, D)), res((n // 2, cr, D))],
        out_shape=[shape_of(m, S, D), shape_of(n // 2, cr, D), shape_of(n // 2, cr, D, dtype=bf16)],
        scratch_shapes=[pltpu.VMEM((SR, 512), bf16), pltpu.VMEM((3 * D, SR), bf16),
                        pltpu.VMEM((3 * D, 512), f32), pltpu.VMEM((8, 2 * D), f32), pltpu.VMEM((n, cr, D), f32)],
        compiler_params=params,
    )(me, x, pt, wt, doT, dx1, g1, b1, qkv)


def swap(v, bit, n):
    return lax.ppermute(v, "dp", [(i, i ^ (1 << bit)) for i in range(n)])


def gather_halves(v, n, bits):
    v = v[None]
    for b in range(1, bits):
        v = jnp.concatenate([v, swap(v, b, n)], axis=0)
    return v, swap(v, 0, n)


def reduce_parts(keep, send, n, bits):
    total = keep + swap(send, 0, n).astype(f32)
    for b in bits:
        half = total.shape[0] // 2
        total = total[:half] + swap(total[half:].astype(bf16), b, n).astype(f32)
    return total[0]


def on_device(n, block_input, first_gain, first_shift, qkv_weight, query_value_bias, proj_weight, proj_bias,
              second_gain, second_shift, up_weight, up_bias, down_weight, down_bias, output_cotangent):
    n_bits = n.bit_length() - 1
    bits = tuple(range(1, n_bits))
    r1, r4 = D // n, FF // n
    me = lax.axis_index("dp").astype(jnp.int32).reshape(1)

    def row(v):
        return v.reshape(1, -1)

    bias = jnp.concatenate([query_value_bias[:D], jnp.zeros((D,), f32), query_value_bias[D:]])
    bias = jnp.broadcast_to(bias[:, None], (3 * D, SL))
    qa, qb = gather_halves(qkv_weight, n, n_bits)
    rest = jnp.concatenate(
        [proj_weight] + [up_weight[:, D * q : D * (q + 1)] for q in range(4)] + [down_weight], axis=0)
    wa, wb = gather_halves(rest, n, n_bits)
    pt, wt, oT, qkv = run_fwd(n, me, qa, qb, block_input, row(first_gain), row(first_shift), bias)
    out, dx1, doT, keep, send = run_mlp(
        n, bits, me, wa, wb, block_input, oT, output_cotangent, row(proj_bias), row(second_gain),
        row(second_shift), row(up_bias), row(down_bias))
    mp = reduce_parts(keep, send, n, bits)
    din, keep, send = run_bwd(n, bits, me, block_input, pt, wt, doT, dx1, row(first_gain), row(first_shift), qkv)
    ap = reduce_parts(keep, send, n, bits)
    g_up = jnp.concatenate([mp[r1 * (1 + q) : r1 * (2 + q)] for q in range(4)], axis=1)
    g_qkv = jnp.concatenate([ap[r1 * q : r1 * (q + 1)] for q in range(3)], axis=1)
    sm, sa = mp[9 * r1], ap[3 * r1]
    return (out, din, sa[:r1], sa[r1 : 2 * r1], g_qkv, sa[2 * r1 : 4 * r1], mp[:r1], sm[2 * r1 : 3 * r1],
            sm[:r1], sm[r1 : 2 * r1], g_up, sm[4 * r1 : 4 * r1 + r4], mp[5 * r1 : 9 * r1], sm[3 * r1 : 4 * r1])


def solution(mesh):
    rows, vec, imgs = P("dp", None), P("dp"), P("dp", None, None)
    n = mesh.shape["dp"]
    return jax.shard_map(
        lambda *args: on_device(n, *args), mesh=mesh,
        in_specs=(imgs, P(), P(), rows, P(), rows, P(), P(), P(), rows, P(), rows, P(), imgs),
        out_specs=(imgs, imgs, vec, vec, rows, vec, rows, vec, vec, vec, rows, vec, rows, vec),
        check_vma=False)
```

```python
import jax
import jax.numpy as jnp
from jax import lax
from jax.experimental import pallas as pl
from jax.experimental.pallas import tpu as pltpu
from jax.sharding import PartitionSpec as P


D = 384
H = 6
FF = 1536
S = 197
SR = 208
SL = 256
CH = 256
NI = 2
FWD_CUT = 14
BWD_CUT = 6
SC = 0.125 * 1.4426950408889634
norm_eps = 1e-06
f32 = jnp.float32
bf16 = jnp.bfloat16
NN = (((1,), (0,)), ((), ()))
NT = (((1,), (1,)), ((), ()))
TN = (((0,), (0,)), ((), ()))


def dot(a, b, dims):
    return lax.dot_general(a, b, dims, preferred_element_type=f32)


def norm(x):
    c = x - jnp.mean(x, axis=-1, keepdims=True)
    r = lax.rsqrt(jnp.mean(c * c, axis=-1, keepdims=True) + norm_eps)
    return c * r, r


def stage_bits(n):
    top = n.bit_length() - 1
    return tuple(range(3, top)) + tuple(range(1, min(3, top)))


def place(k, n):
    return sum(((k >> b) & 1) << i for i, b in enumerate(stage_bits(n)))


def rest_rows(n):
    return -(-9 * (D // n) // 16) * 16


def for_parity(me, body):
    for parity in (0, 1):
        @pl.when((me & 1) == parity)
        def _():
            body(parity)


def attn_fwd(me_ref, *refs, n, lead):
    if lead:
        ga_ref, gb_ref, x_ref, g_ref, b_ref, bias_ref, pt_ref, wt_ref, ot_ref, wT_s, a_s, w_s = refs
    else:
        wT_s, x_ref, g_ref, b_ref, bias_ref, _, _, _, pt_ref, wt_ref, ot_ref, a_s = refs

    @pl.when(pl.program_id(0) == 0)
    def _():
        a_s[...] = jnp.zeros_like(a_s)
        if lead:
            me = me_ref[0]
            r1 = D // n

            def gather(parity):
                for k in range(n):
                    src = ga_ref if (k & 1) == parity else gb_ref
                    p = place(k, n)
                    w_s[r1 * k : r1 * (k + 1), :] = src[r1 * p : r1 * (p + 1), :]

            for_parity(me, gather)
            wT_s[...] = w_s[...].T

    valid = lax.broadcasted_iota(jnp.int32, (16, SL), 0) < S - 192

    def ln(i):
        n1, _ = norm(x_ref[i].astype(f32))
        a_s[i, :S, :] = (n1 * g_ref[...] + b_ref[...]).astype(bf16)

    def proj(i):
        pT = dot(wT_s[...], a_s[i], NT) + bias_ref[...]
        pt_ref[i] = pT.astype(bf16)

    def soft(i, h):
        qT = pt_ref[i, 64 * h : 64 * h + 64, :]
        kT = pt_ref[i, D + 64 * h : D + 64 * h + 64, :SR]
        z = dot(kT, qT, TN)
        zt = z[:192]
        zb = jnp.where(valid, z[192:], -jnp.inf)
        m = jnp.maximum(jnp.max(zt, axis=0, keepdims=True), jnp.max(zb, axis=0, keepdims=True))
        et = jnp.exp2((zt - m) * SC)
        eb = jnp.exp2((zb - m) * SC)
        l = jnp.sum(et, axis=0, keepdims=True) + jnp.sum(eb, axis=0, keepdims=True)
        inv = 1.0 / l
        wt_ref[i, h, :192, :] = (et * inv).astype(bf16)
        wt_ref[i, h, 192:, :] = (eb * inv).astype(bf16)

    def pv(i, h):
        vT = pt_ref[i, 2 * D + 64 * h : 2 * D + 64 * h + 64, :SR]
        ot_ref[i, 64 * h : 64 * h + 64, :] = dot(vT, wt_ref[i, h], NN).astype(bf16)

    for i in range(NI): ln(i)
    for i in range(NI): proj(i)
    for i in range(NI):
        for h in range(H):
            soft(i, h)
            if i > 0: pv(i - 1, h)
    for h in range(H): pv(NI - 1, h)


ERF_P = 0.3275911
ERF_A = (0.254829592, -0.284496736, 1.421413741, -1.453152027, 1.061405429)


def gelu_parts(u):
    e = jnp.exp2(u * u * (-0.5 * 1.4426950408889634))
    t = 1.0 / (1.0 + jnp.abs(u) * (ERF_P * 0.7071067811865476))
    poly = ERF_A[4] * 0.5
    for a in ERF_A[3::-1]:
        poly = poly * t + a * 0.5
    q = poly * t * e
    phi = jnp.where(u >= 0, 1.0 - q, q)
    return u * phi, phi + u * (e * 0.3989422804014327)


def spread(vec, width, shift, n):
    size = n * width
    d = lax.broadcasted_iota(jnp.int32, (n, size), 1)
    k = lax.broadcasted_iota(jnp.int32, (n, size), 0)
    picked = jnp.where(d // width == k, jnp.broadcast_to(vec, (n, size)), 0.0).astype(bf16)
    dd = lax.broadcasted_iota(jnp.int32, (size, 128), 0)
    j = lax.broadcasted_iota(jnp.int32, (size, 128), 1)
    place = jnp.where(dd % width + shift == j, 1.0, 0.0).astype(bf16)
    return dot(picked, place, NN)


def emit(me, stage, keep_ref, send_ref, n, bits):
    def one(k, carry):
        m = me ^ k
        pos = 0
        for b in bits:
            pos = pos * 2 + ((m >> b) & 1)

        @pl.when((m & 1) == 0)
        def _():
            keep_ref[pos] = stage[k]

        @pl.when((m & 1) == 1)
        def _():
            send_ref[pos] = stage[k].astype(bf16)

        return carry

    lax.fori_loop(0, n, one, 0)


def mlp(me_ref, ga_ref, gb_ref, x_ref, ot_ref, e_ref, pb_ref, g_ref, b_ref, ub_ref, db_ref,
        out_ref, dx1_ref, dot_ref, keep_ref, send_ref,
        xs, es, fs, pj_s, up_s, dn_s, gup, gdn, gpj, small, stage, upT, dnT, gs, us, bt, *, n, bits):
    me = me_ref[0]
    step = pl.program_id(0)
    r1, r4 = D // n, FF // n
    rw = rest_rows(n)

    @pl.when(step == 0)
    def _():
        xs[...] = jnp.zeros_like(xs)
        es[...] = jnp.zeros_like(es)
        fs[...] = jnp.zeros_like(fs)
        gup[...] = jnp.zeros_like(gup)
        gdn[...] = jnp.zeros_like(gdn)
        gpj[...] = jnp.zeros_like(gpj)
        small[...] = jnp.zeros_like(small)
        bt[:, D:, :] = jnp.ones((NI, 16, SR), bf16)

        def gather(parity):
            for k in range(n):
                src = ga_ref if (k & 1) == parity else gb_ref
                p = place(k, n)
                part = src[rw * p : rw * (p + 1), :]
                rows = slice(r1 * k, r1 * (k + 1))
                pj_s[rows, :] = part[:r1]
                for q in range(4):
                    up_s[rows, D * q : D * (q + 1)] = part[r1 * (1 + q) : r1 * (2 + q)]
                dn_s[r4 * k : r4 * (k + 1), :] = part[5 * r1 : 9 * r1]

        for_parity(me, gather)
        upT[...] = up_s[...].T
        dnT[...] = dn_s[...].T

    def fold(v):
        return jnp.sum(v.reshape(SR // 8, 8, v.shape[1]), axis=0)

    st = [dict() for _ in range(NI)]

    def p1(i):
        s = st[i]
        xs[i, :S, :] = x_ref[i]
        es[i, :S, :] = e_ref[i]
        s["oT"] = ot_ref[i, :, :SR]
        s["x1"] = xs[i].astype(f32) + dot(s["oT"], pj_s[...], TN) + pb_ref[...]
        s["n2"], s["r2"] = norm(s["x1"])
        bb = (s["n2"] * g_ref[...] + b_ref[...]).astype(bf16)
        s["bb"] = bb
        bt[i, :D, :] = bb.T
        s["eT"] = es[i].T

    def p2(i, c):
        cols = slice(c * CH, (c + 1) * CH)
        u = dot(st[i]["bb"], up_s[:, cols], NN) + ub_ref[:, cols]
        g, gp = gelu_parts(u)
        gs[i, :, cols] = g.astype(bf16)
        us[i, :, cols] = (dot(es[i], dnT[:, cols], NN) * gp).astype(bf16)

    def p3(i, c):
        cols = slice(c * CH, (c + 1) * CH)
        gdn[:, cols] += dot(st[i]["eT"], gs[i, :, cols], NN)
        gup[:, cols] += dot(bt[i], us[i, :, cols], NN)

    def p4(i):
        s = st[i]
        s["dB"] = dot(us[i], upT[...], NN)
        out_ref[i] = (s["x1"] + db_ref[...] + dot(gs[i], dn_s[...], NN))[:S]

    def p5(i):
        s = st[i]
        dB, n2 = s["dB"], s["n2"]
        dn = dB * g_ref[...]
        ef = es[i].astype(f32)
        dx1 = ef + s["r2"] * (dn - jnp.mean(dn, axis=-1, keepdims=True) - n2 * jnp.mean(dn * n2, axis=-1, keepdims=True))
        dx1_ref[i] = dx1[:S]
        ff = dx1.astype(bf16)
        fs[i, :SR, :] = ff
        small[0:8, 0:384] += fold(dB * n2)
        small[0:8, 384:768] += fold(dB)
        small[0:8, 768:1152] += fold(ff.astype(f32))
        small[0:8, 1152:1536] += fold(ef)

    def p6(i):
        gpj[...] += dot(st[i]["oT"], fs[i, :SR, :], NN)
        dot_ref[i] = dot(pj_s[...], fs[i], NT).astype(bf16)

    C = FF // CH
    p1(0)
    p1(1)
    for c in range(C): p2(0, c)
    for c in range(C):
        p2(1, c)
        p3(0, c)
    p4(0)
    p4(1)
    p5(0)
    for c in range(C // 2): p3(1, c)
    p6(0)
    p5(1)
    for c in range(C // 2, C): p3(1, c)
    p6(1)

    @pl.when(step == pl.num_programs(0) - 1)
    def _():
        tot = jnp.sum(small[...], axis=0, keepdims=True)
        sm = spread(gup[D : D + 1, :], r4, 4 * r1, n)
        for q in range(4):
            sm = sm + spread(tot[:, D * q : D * (q + 1)], r1, r1 * q, n)
        for k in range(n):
            rows = slice(r1 * k, r1 * (k + 1))
            stage[k, :r1, :] = gpj[rows, :]
            for q in range(4):
                stage[k, r1 * (1 + q) : r1 * (2 + q), :] = gup[rows, D * q : D * (q + 1)]
            stage[k, 9 * r1 : 9 * r1 + 1, :128] = sm[k : k + 1]
        for c in range(FF // 384):
            gT = gdn[:, 384 * c : 384 * (c + 1)].T
            for k in range(384 // r4):
                stage[c * (384 // r4) + k, 5 * r1 : 9 * r1, :] = gT[r4 * k : r4 * (k + 1)]
        emit(me, stage, keep_ref, send_ref, n, bits)


def attn_bwd(me_ref, x_ref, pt_ref, wt_ref, dot_ref, dx1_ref, g_ref, b_ref, wT_s, *refs, n, bits, lead, last):
    if not lead:
        gqi_ref, smi_ref, _ = refs[:3]
        refs = refs[3:]
    if last:
        din_ref, keep_ref, send_ref, as_, dp_s, dz_s, gq, small, stage = refs
    else:
        din_ref, gq, small, as_, dp_s, dz_s = refs
    step = pl.program_id(0)

    @pl.when(step == 0)
    def _():
        as_[:, :, :D] = jnp.zeros((NI, SR, D), bf16)
        as_[:, :, D:] = jnp.ones((NI, SR, 128), bf16)
        gq[...] = jnp.zeros_like(gq) if lead else gqi_ref[...]
        small[...] = jnp.zeros_like(small) if lead else smi_ref[...]

    hs = [slice(64 * h, 64 * h + 64) for h in range(H)]
    ks = [slice(D + 64 * h, D + 64 * h + 64) for h in range(H)]
    vs = [slice(2 * D + 64 * h, 2 * D + 64 * h + 64) for h in range(H)]
    st = [dict() for _ in range(NI)]

    def ln(i):
        n1, r1 = norm(x_ref[i].astype(f32))
        st[i].update(n1=n1, r1=r1)
        as_[i, :S, :D] = (n1 * g_ref[...] + b_ref[...]).astype(bf16)

    def dz(i, h):
        w = wt_ref[i, h].astype(f32)
        t = dot(pt_ref[i, vs[h], :SR], dot_ref[i, hs[h], :], TN) * w
        dz_s[i, h] = (t - w * jnp.sum(t, axis=0, keepdims=True)).astype(bf16)

    def dv(i, h):
        dp_s[i, vs[h], :] = dot(dot_ref[i, hs[h], :], wt_ref[i, h], NT).astype(bf16)

    def dq(i, h):
        dp_s[i, hs[h], :] = (dot(pt_ref[i, ks[h], :SR], dz_s[i, h], NN) * 0.125)[:, :SR].astype(bf16)

    def dk(i, h):
        dp_s[i, ks[h], :] = (dot(pt_ref[i, hs[h], :], dz_s[i, h], NT) * 0.125).astype(bf16)

    def gr(i):
        st[i]["dA"] = dot(dp_s[i], wT_s[...], TN)[:S]
        gq[...] += dot(dp_s[i], as_[i], NN)

    def fin(i):
        n1, r1, dA = st[i]["n1"], st[i]["r1"], st[i]["dA"]
        dm = dA * g_ref[...]
        din_ref[i] = dx1_ref[i] + r1 * (
            dm - jnp.mean(dm, axis=-1, keepdims=True) - n1 * jnp.mean(dm * n1, axis=-1, keepdims=True))
        small[0:1, 0:384] += jnp.sum(dA * n1, axis=0, keepdims=True)
        small[0:1, 384:768] += jnp.sum(dA, axis=0, keepdims=True)

    for i in range(NI): ln(i)
    for h in range(H): dz(0, h)
    for h in range(H):
        dz(1, h)
        dv(0, h)
        dq(0, h)
        dk(0, h)
    for h in range(H):
        dv(1, h)
        dq(1, h)
        dk(1, h)
    gr(0)
    gr(1)
    fin(0)
    fin(1)

    if last:
        @pl.when(step == pl.num_programs(0) - 1)
        def _():
            me = me_ref[0]
            r1 = D // n
            cs = gq[:, D : D + 128].T[0:1, :]
            sm = spread(small[0:1, :D], r1, 0, n) + spread(small[0:1, D : 2 * D], r1, r1, n)
            sm = sm + spread(jnp.concatenate([cs[:, :D], cs[:, 2 * D :]], axis=1), 2 * r1, 2 * r1, n)
            for q in range(3):
                gT = gq[D * q : D * (q + 1), :D].T
                for k in range(n):
                    stage[k, r1 * q : r1 * (q + 1), :] = gT[r1 * k : r1 * (k + 1)]
            for k in range(n):
                stage[k, 3 * r1 : 3 * r1 + 1, :128] = sm[k : k + 1]
            emit(me, stage, keep_ref, send_ref, n, bits)


def img(shape, at=0):
    return pl.BlockSpec((NI,) + shape, lambda i: (i + at // NI,) + (0,) * len(shape))


def res(shape):
    return pl.BlockSpec(shape, lambda i: (0,) * len(shape))


smem = pl.BlockSpec(memory_space=pltpu.SMEM)
hbm = pl.BlockSpec(memory_space=pl.ANY)
params = pltpu.CompilerParams(dimension_semantics=("arbitrary",), vmem_limit_bytes=60 * 2**20)


def shape_of(*dims, dtype=f32):
    return jax.ShapeDtypeStruct(dims, dtype)


def vmem(*dims, dtype=bf16):
    return pltpu.VMEM(dims, dtype)


def run_fwd(n, me, weights, x, g1, b1, bias, at, count, kept=()):
    m = x.shape[0]
    lead = not kept
    out_specs = [img((3 * D, SL), at), img((H, SR, SL), at), img((D, SL), at)]
    out_shape = [shape_of(m, 3 * D, SL, dtype=bf16), shape_of(m, H, SR, SL, dtype=bf16), shape_of(m, D, SL, dtype=bf16)]
    scratch = [vmem(NI, SL, D)]
    if lead:
        out_specs, out_shape = out_specs + [res((3 * D, D))], out_shape + [shape_of(3 * D, D, dtype=bf16)]
        scratch = scratch + [vmem(D, 3 * D)]
    base = 1 + len(weights) + 4
    return pl.pallas_call(
        lambda *refs: attn_fwd(*refs, n=n, lead=lead), grid=(count // NI,), name="attn_fwd",
        in_specs=[smem] + [res(w.shape) for w in weights] + [img((S, D), at), res((1, D)), res((1, D)), res((3 * D, SL))]
        + [hbm] * len(kept),
        out_specs=out_specs, out_shape=out_shape, scratch_shapes=scratch,
        input_output_aliases={base + i: i for i in range(len(kept))},
        compiler_params=params,
    )(me, *weights, x, g1, b1, bias, *kept)


def chunk_rows(n, parts):
    return -(-(parts * (D // n) + 1) // 16) * 16


def run_mlp(n, bits, me, ga, gb, x, oT, e, pb, g2, b2, ub, db):
    m = x.shape[0]
    cr = chunk_rows(n, 9)
    return pl.pallas_call(
        lambda *refs: mlp(*refs, n=n, bits=bits), grid=(m // NI,), name="mlp",
        in_specs=[smem, res(ga.shape), res(gb.shape), img((S, D)), img((D, SL)), img((S, D)),
                  res((1, D)), res((1, D)), res((1, D)), res((1, FF)), res((1, D))],
        out_specs=[img((S, D)), img((S, D)), img((D, SL)), res((n // 2, cr, D)), res((n // 2, cr, D))],
        out_shape=[shape_of(m, S, D), shape_of(m, S, D), shape_of(m, D, SL, dtype=bf16),
                   shape_of(n // 2, cr, D), shape_of(n // 2, cr, D, dtype=bf16)],
        scratch_shapes=[vmem(NI, SR, D), vmem(NI, SR, D), vmem(NI, SL, D), vmem(D, D), vmem(D, FF), vmem(FF, D),
                        vmem(D + 16, FF, dtype=f32), vmem(D, FF, dtype=f32), vmem(D, D, dtype=f32),
                        vmem(8, FF, dtype=f32), vmem(n, cr, D, dtype=f32), vmem(FF, D), vmem(D, FF),
                        vmem(NI, SR, FF), vmem(NI, SR, FF), vmem(NI, D + 16, SR)],
        compiler_params=params,
    )(me, ga, gb, x, oT, e, pb, g2, b2, ub, db)


def run_bwd(n, bits, me, x, pt, wt, doT, dx1, g1, b1, wT, at, count, kept=()):
    m = x.shape[0]
    cr = chunk_rows(n, 3)
    lead, last = not kept, at + count == m
    out_specs, out_shape = [img((S, D), at)], [shape_of(m, S, D)]
    scratch = [vmem(NI, SR, 512), vmem(NI, 3 * D, SR), vmem(NI, H, SR, SL)]
    sums = [((3 * D, 512), f32), ((8, 2 * D), f32)]
    if last:
        out_specs = out_specs + [res((n // 2, cr, D))] * 2
        out_shape = out_shape + [shape_of(n // 2, cr, D), shape_of(n // 2, cr, D, dtype=bf16)]
        scratch = scratch + [vmem(*s, dtype=t) for s, t in sums] + [vmem(n, cr, D, dtype=f32)]
    else:
        out_specs = out_specs + [res(s) for s, _ in sums]
        out_shape = out_shape + [shape_of(*s, dtype=t) for s, t in sums]
    return pl.pallas_call(
        lambda *refs: attn_bwd(*refs, n=n, bits=bits, lead=lead, last=last), grid=(count // NI,), name="attn_bwd",
        in_specs=[smem, img((S, D), at), img((3 * D, SL), at), img((H, SR, SL), at), img((D, SL), at), img((S, D), at),
                  res((1, D)), res((1, D)), res((3 * D, D))]
        + ([] if lead else [res(s) for s, _ in sums] + [hbm]),
        out_specs=out_specs, out_shape=out_shape, scratch_shapes=scratch,
        input_output_aliases={} if lead else {11: 0},
        compiler_params=params,
    )(me, x, pt, wt, doT, dx1, g1, b1, wT, *kept)


def swap(v, bit, n):
    return lax.ppermute(v, "dp", [(i, i ^ (1 << bit)) for i in range(n)])


def gather_halves(v, me, n):
    bits = stage_bits(n)
    for b in bits:
        other = swap(v, b, n)
        high = (me >> b) & 1 == 1
        v = jnp.where(high, jnp.concatenate([other, v], axis=0), jnp.concatenate([v, other], axis=0))
    return v, swap(v, 0, n)


def reduce_parts(keep, send, n, bits):
    got = swap(send, 0, n)
    total = keep + got.astype(f32)
    for b in bits:
        half = total.shape[0] // 2
        part = total[half:].astype(bf16)
        got = swap(part, b, n)
        total = total[:half] + got.astype(f32)
    return total[0]


def on_device(n, block_input, first_gain, first_shift, qkv_weight, query_value_bias, proj_weight, proj_bias,
              second_gain, second_shift, up_weight, up_bias, down_weight, down_bias, output_cotangent):
    n_bits = n.bit_length() - 1
    bits = tuple(range(1, n_bits))
    r1, r4 = D // n, FF // n
    at = lax.axis_index("dp").astype(jnp.int32)
    me = at.reshape(1)

    def row(v):
        return v.reshape(1, -1)

    bias = jnp.concatenate([query_value_bias[:D], jnp.zeros((D,), f32), query_value_bias[D:]])
    bias = jnp.broadcast_to(bias[:, None], (3 * D, SL))
    qa, qb = gather_halves(qkv_weight, at, n)
    rest = jnp.concatenate(
        [proj_weight] + [up_weight[:, D * q : D * (q + 1)] for q in range(4)] + [down_weight]
        + [jnp.zeros((rest_rows(n) - 9 * r1, D), bf16)], axis=0)
    wa, wb = gather_halves(rest, at, n)
    m = block_input.shape[0]
    norm1 = (row(first_gain), row(first_shift))
    cut = FWD_CUT
    *acts, wT = run_fwd(n, me, (qa, qb), block_input, *norm1, bias, 0, cut)
    pt, wt, oT = run_fwd(n, me, (wT,), block_input, *norm1, bias, cut, m - cut, acts)
    out, dx1, doT, keep, send = run_mlp(
        n, bits, me, wa, wb, block_input, oT, output_cotangent, row(proj_bias), row(second_gain),
        row(second_shift), row(up_bias), row(down_bias))
    mp = reduce_parts(keep, send, n, bits)
    cut = BWD_CUT
    dins, gq, sm = run_bwd(n, bits, me, block_input, pt, wt, doT, dx1, *norm1, wT, 0, cut)
    din, keep, send = run_bwd(n, bits, me, block_input, pt, wt, doT, dx1, *norm1, wT, cut, m - cut, (gq, sm, dins))
    ap = reduce_parts(keep, send, n, bits)
    g_up = jnp.concatenate([mp[r1 * (1 + q) : r1 * (2 + q)] for q in range(4)], axis=1)
    g_qkv = jnp.concatenate([ap[r1 * q : r1 * (q + 1)] for q in range(3)], axis=1)
    sm, sa = mp[9 * r1], ap[3 * r1]
    return (out, din, sa[:r1], sa[r1 : 2 * r1], g_qkv, sa[2 * r1 : 4 * r1], mp[:r1], sm[2 * r1 : 3 * r1],
            sm[:r1], sm[r1 : 2 * r1], g_up, sm[4 * r1 : 4 * r1 + r4], mp[5 * r1 : 9 * r1], sm[3 * r1 : 4 * r1])


def solution(mesh):
    rows, vec, imgs = P("dp", None), P("dp"), P("dp", None, None)
    n = mesh.shape["dp"]

    def body(*args):
        return on_device(n, *args)

    return jax.shard_map(
        body, mesh=mesh,
        in_specs=(imgs, P(), P(), rows, P(), rows, P(), P(), P(), rows, P(), rows, P(), imgs),
        out_specs=(imgs, imgs, vec, vec, rows, vec, rows, vec, vec, vec, rows, vec, rows, vec),
        check_vma=False)
```

```python
import jax
import jax.numpy as jnp
from jax import lax
from jax.experimental import pallas as pl
from jax.experimental.pallas import tpu as pltpu
from jax.sharding import PartitionSpec as P


D = 384
H = 6
FF = 1536
S = 197
SR = 208
SL = 256
CH = 256
NI = 2
NF = 4
FWD_CUTS = (16,)
BWD_CUTS = (4,)
SC = 0.125 * 1.4426950408889634
norm_eps = 1e-06
f32 = jnp.float32
bf16 = jnp.bfloat16
NN = (((1,), (0,)), ((), ()))
NT = (((1,), (1,)), ((), ()))
TN = (((0,), (0,)), ((), ()))


def dot(a, b, dims):
    return lax.dot_general(a, b, dims, preferred_element_type=f32)


def norm(x):
    c = x - jnp.mean(x, axis=-1, keepdims=True)
    r = lax.rsqrt(jnp.mean(c * c, axis=-1, keepdims=True) + norm_eps)
    return c * r, r


def stage_bits(n):
    top = n.bit_length() - 1
    return tuple(range(3, top)) + tuple(range(1, min(3, top)))


def place(k, n):
    return sum(((k >> b) & 1) << i for i, b in enumerate(stage_bits(n)))


def rest_rows(n):
    return -(-9 * (D // n) // 16) * 16


def for_parity(me, body):
    for parity in (0, 1):
        @pl.when((me & 1) == parity)
        def _():
            body(parity)


def row(v_ref):
    return v_ref[...].reshape(1, -1)


def attn_fwd(g_ref, b_ref, qv_ref, *refs, n, lead):
    if lead:
        me_ref, ga_ref, gb_ref, x_ref, pt_ref, wt_ref, ot_ref, wT_s, bias, a_s, w_s = refs
    else:
        wT_s, x_ref, _, _, _, pt_ref, wt_ref, ot_ref, bias, a_s = refs

    @pl.when(pl.program_id(0) == 0)
    def _():
        a_s[...] = jnp.zeros_like(a_s)
        bias[D : 2 * D, :] = jnp.zeros((D, SL), f32)
        for q in (0, 1):
            col = jnp.broadcast_to(qv_ref[D * q : D * (q + 1)].reshape(1, D), (8, D)).T[:, 0:1]
            bias[2 * D * q : 2 * D * q + D, :] = jnp.broadcast_to(col, (D, SL))
        if lead:
            r1 = D // n

            def gather(parity):
                for k in range(n):
                    src = ga_ref if (k & 1) == parity else gb_ref
                    p = place(k, n)
                    w_s[r1 * k : r1 * (k + 1), :] = src[r1 * p : r1 * (p + 1), :]

            for_parity(me_ref[0], gather)
            wT_s[...] = w_s[...].T

    valid = lax.broadcasted_iota(jnp.int32, (16, SL), 0) < S - 192

    def ln(i):
        n1, _ = norm(x_ref[i].astype(f32))
        a_s[i, :S, :] = (n1 * row(g_ref) + row(b_ref)).astype(bf16)

    def proj(i):
        pt_ref[i] = (dot(wT_s[...], a_s[i], NT) + bias[...]).astype(bf16)

    def soft(i, h):
        qT = pt_ref[i, 64 * h : 64 * h + 64, :]
        kT = pt_ref[i, D + 64 * h : D + 64 * h + 64, :SR]
        z = dot(kT, qT, TN)
        zt = z[:192]
        zb = jnp.where(valid, z[192:], -jnp.inf)
        m = jnp.maximum(jnp.max(zt, axis=0, keepdims=True), jnp.max(zb, axis=0, keepdims=True))
        et = jnp.exp2((zt - m) * SC)
        eb = jnp.exp2((zb - m) * SC)
        l = jnp.sum(et, axis=0, keepdims=True) + jnp.sum(eb, axis=0, keepdims=True)
        inv = 1.0 / l
        wt_ref[i, h, :192, :] = (et * inv).astype(bf16)
        wt_ref[i, h, 192:, :] = (eb * inv).astype(bf16)

    def pv(i, h):
        vT = pt_ref[i, 2 * D + 64 * h : 2 * D + 64 * h + 64, :SR]
        ot_ref[i, 64 * h : 64 * h + 64, :] = dot(vT, wt_ref[i, h], NN).astype(bf16)

    for i in range(NF):
        ln(i)
    for i in range(NF):
        proj(i)
    for i in range(NF):
        for h in range(H):
            soft(i, h)
            if i > 0:
                pv(i - 1, h)
    for h in range(H):
        pv(NF - 1, h)


ERF_P = 0.3275911
ERF_A = (0.254829592, -0.284496736, 1.421413741, -1.453152027, 1.061405429)


def gelu_parts(u):
    e = jnp.exp2(u * u * (-0.5 * 1.4426950408889634))
    t = 1.0 / (1.0 + jnp.abs(u) * (ERF_P * 0.7071067811865476))
    poly = ERF_A[4] * 0.5
    for a in ERF_A[3::-1]:
        poly = poly * t + a * 0.5
    q = poly * t * e
    phi = jnp.where(u >= 0, 1.0 - q, q)
    return u * phi, phi + u * (e * 0.3989422804014327)


def spread(vec, width, shift, n):
    size = n * width
    d = lax.broadcasted_iota(jnp.int32, (n, size), 1)
    k = lax.broadcasted_iota(jnp.int32, (n, size), 0)
    picked = jnp.where(d // width == k, jnp.broadcast_to(vec, (n, size)), 0.0).astype(bf16)
    dd = lax.broadcasted_iota(jnp.int32, (size, 128), 0)
    j = lax.broadcasted_iota(jnp.int32, (size, 128), 1)
    place = jnp.where(dd % width + shift == j, 1.0, 0.0).astype(bf16)
    return dot(picked, place, NN)


def emit(me, stage, keep_ref, send_ref, n, bits):
    def one(k, carry):
        m = me ^ k
        pos = 0
        for b in bits:
            pos = pos * 2 + ((m >> b) & 1)

        @pl.when((m & 1) == 0)
        def _():
            keep_ref[pos] = stage[k]

        @pl.when((m & 1) == 1)
        def _():
            send_ref[pos] = stage[k].astype(bf16)

        return carry

    lax.fori_loop(0, n, one, 0)


def mlp(pb_ref, g_ref, b_ref, ub_ref, db_ref, me_ref, ga_ref, gb_ref, x_ref, ot_ref, e_ref,
        out_ref, dx1_ref, dot_ref, keep_ref, send_ref,
        xs, es, fs, pj_s, up_s, dn_s, gup, gdn, gpj, small, stage, upT, dnT, gs, us, bt, ub_s, *, n, bits):
    me = me_ref[0]
    step = pl.program_id(0)
    r1, r4 = D // n, FF // n
    rw = rest_rows(n)

    @pl.when(step == 0)
    def _():
        xs[...] = jnp.zeros_like(xs)
        es[...] = jnp.zeros_like(es)
        fs[...] = jnp.zeros_like(fs)
        gup[...] = jnp.zeros_like(gup)
        gdn[...] = jnp.zeros_like(gdn)
        gpj[...] = jnp.zeros_like(gpj)
        small[...] = jnp.zeros_like(small)
        for q in range(4):
            ub_s[:, D * q : D * (q + 1)] = ub_ref[D * q : D * (q + 1)].reshape(1, D)
        bt[:, D:, :] = jnp.ones((NI, 16, SR), bf16)

        def gather(parity):
            for k in range(n):
                src = ga_ref if (k & 1) == parity else gb_ref
                p = place(k, n)
                part = src[rw * p : rw * (p + 1), :]
                rows = slice(r1 * k, r1 * (k + 1))
                pj_s[rows, :] = part[:r1]
                for q in range(4):
                    up_s[rows, D * q : D * (q + 1)] = part[r1 * (1 + q) : r1 * (2 + q)]
                dn_s[r4 * k : r4 * (k + 1), :] = part[5 * r1 : 9 * r1]

        for_parity(me, gather)
        upT[...] = up_s[...].T
        dnT[...] = dn_s[...].T

    def fold(v):
        return jnp.sum(v.reshape(SR // 8, 8, v.shape[1]), axis=0)

    st = [dict() for _ in range(NI)]

    def p1(i):
        s = st[i]
        xs[i, :S, :] = x_ref[i]
        es[i, :S, :] = e_ref[i]
        s["oT"] = ot_ref[i, :, :SR]
        s["x1"] = xs[i].astype(f32) + dot(s["oT"], pj_s[...], TN) + row(pb_ref)
        s["n2"], s["r2"] = norm(s["x1"])
        bb = (s["n2"] * row(g_ref) + row(b_ref)).astype(bf16)
        s["bb"] = bb
        bt[i, :D, :] = bb.T
        s["eT"] = es[i].T

    def p2(i, c):
        cols = slice(c * CH, (c + 1) * CH)
        u = dot(st[i]["bb"], up_s[:, cols], NN) + ub_s[:, cols]
        g, gp = gelu_parts(u)
        gs[i, :, cols] = g.astype(bf16)
        us[i, :, cols] = (dot(es[i], dnT[:, cols], NN) * gp).astype(bf16)

    def p3(i, c):
        cols = slice(c * CH, (c + 1) * CH)
        gdn[:, cols] += dot(st[i]["eT"], gs[i, :, cols], NN)
        gup[:, cols] += dot(bt[i], us[i, :, cols], NN)

    def p4(i):
        s = st[i]
        s["dB"] = dot(us[i], upT[...], NN)
        out_ref[i] = (s["x1"] + row(db_ref) + dot(gs[i], dn_s[...], NN))[:S]

    def p5(i):
        s = st[i]
        dB, n2 = s["dB"], s["n2"]
        dn = dB * row(g_ref)
        ef = es[i].astype(f32)
        dx1 = ef + s["r2"] * (dn - jnp.mean(dn, axis=-1, keepdims=True) - n2 * jnp.mean(dn * n2, axis=-1, keepdims=True))
        dx1_ref[i] = dx1[:S]
        ff = dx1.astype(bf16)
        fs[i, :SR, :] = ff
        small[:, 0:384] += fold(dB * n2)
        small[:, 384:768] += fold(dB)
        small[:, 768:1152] += fold(ff.astype(f32))
        small[:, 1152:1536] += fold(ef)

    def p6(i):
        gpj[...] += dot(st[i]["oT"], fs[i, :SR, :], NN)
        dot_ref[i] = dot(pj_s[...], fs[i], NT).astype(bf16)

    C = FF // CH
    p1(0)
    p1(1)
    for c in range(C): p2(0, c)
    for c in range(C):
        p2(1, c)
        p3(0, c)
    p4(0)
    p4(1)
    p5(0)
    for c in range(C // 2): p3(1, c)
    p6(0)
    p5(1)
    for c in range(C // 2, C): p3(1, c)
    p6(1)

    @pl.when(step == pl.num_programs(0) - 1)
    def _():
        tot = jnp.sum(small[...], axis=0, keepdims=True)
        sm = spread(gup[D : D + 1, :], r4, 4 * r1, n)
        for q in range(4):
            sm = sm + spread(tot[:, D * q : D * (q + 1)], r1, r1 * q, n)
        for k in range(n):
            rows = slice(r1 * k, r1 * (k + 1))
            stage[k, :r1, :] = gpj[rows, :]
            for q in range(4):
                stage[k, r1 * (1 + q) : r1 * (2 + q), :] = gup[rows, D * q : D * (q + 1)]
            stage[k, 9 * r1 : 9 * r1 + 1, :128] = sm[k : k + 1]
        for c in range(FF // 384):
            gT = gdn[:, 384 * c : 384 * (c + 1)].T
            for k in range(384 // r4):
                stage[c * (384 // r4) + k, 5 * r1 : 9 * r1, :] = gT[r4 * k : r4 * (k + 1)]
        emit(me, stage, keep_ref, send_ref, n, bits)


def attn_bwd(g_ref, b_ref, me_ref, x_ref, pt_ref, wt_ref, dot_ref, dx1_ref, wT_ref, *refs, n, bits, lead, last):
    if not lead:
        gqi_ref, smi_ref, _ = refs[:3]
        refs = refs[3:]
    if last:
        din_ref, keep_ref, send_ref, as_, dp_s, dz_s, gq, small, stage = refs
    else:
        din_ref, gq, small, as_, dp_s, dz_s = refs
    step = pl.program_id(0)

    @pl.when(step == 0)
    def _():
        as_[:, :, :D] = jnp.zeros((NI, SR, D), bf16)
        as_[:, :, D:] = jnp.ones((NI, SR, 128), bf16)
        gq[...] = jnp.zeros_like(gq) if lead else gqi_ref[...]
        small[...] = jnp.zeros_like(small) if lead else smi_ref[...]

    hs = [slice(64 * h, 64 * h + 64) for h in range(H)]
    ks = [slice(D + 64 * h, D + 64 * h + 64) for h in range(H)]
    vs = [slice(2 * D + 64 * h, 2 * D + 64 * h + 64) for h in range(H)]
    st = [dict() for _ in range(NI)]

    def ln(i):
        n1, r1 = norm(x_ref[i].astype(f32))
        st[i].update(n1=n1, r1=r1)
        as_[i, :S, :D] = (n1 * row(g_ref) + row(b_ref)).astype(bf16)

    def dz(i, h):
        w = wt_ref[i, h].astype(f32)
        t = dot(pt_ref[i, vs[h], :SR], dot_ref[i, hs[h], :], TN) * w
        dz_s[i, h] = (t - w * jnp.sum(t, axis=0, keepdims=True)).astype(bf16)

    def dv(i, h):
        dp_s[i, vs[h], :] = dot(dot_ref[i, hs[h], :], wt_ref[i, h], NT).astype(bf16)

    def dq(i, h):
        dp_s[i, hs[h], :] = (dot(pt_ref[i, ks[h], :SR], dz_s[i, h], NN) * 0.125)[:, :SR].astype(bf16)

    def dk(i, h):
        dp_s[i, ks[h], :] = (dot(pt_ref[i, hs[h], :], dz_s[i, h], NT) * 0.125).astype(bf16)

    def gr(i):
        st[i]["dA"] = dot(dp_s[i], wT_ref[...], TN)[:S]
        gq[...] += dot(dp_s[i], as_[i], NN)

    def fin(i):
        n1, r1, dA = st[i]["n1"], st[i]["r1"], st[i]["dA"]
        dm = dA * row(g_ref)
        din_ref[i] = dx1_ref[i] + r1 * (
            dm - jnp.mean(dm, axis=-1, keepdims=True) - n1 * jnp.mean(dm * n1, axis=-1, keepdims=True))
        small[0:1, 0:D] += jnp.sum(dA * n1, axis=0, keepdims=True)
        small[0:1, D : 2 * D] += jnp.sum(dA, axis=0, keepdims=True)

    for i in range(NI):
        ln(i)
    for i in range(NI + 1):
        for h in range(H):
            if i < NI:
                dz(i, h)
            if i > 0:
                dv(i - 1, h)
                dq(i - 1, h)
                dk(i - 1, h)
        if i > 1:
            gr(i - 2)
        if i > 2:
            fin(i - 3)
    gr(NI - 1)
    if NI > 1:
        fin(NI - 2)
    fin(NI - 1)

    if last:
        @pl.when(step == pl.num_programs(0) - 1)
        def _():
            me = me_ref[0]
            r1 = D // n
            cs = gq[:, D : D + 128].T[0:1, :]
            sm = spread(small[0:1, :D], r1, 0, n) + spread(small[0:1, D : 2 * D], r1, r1, n)
            sm = sm + spread(jnp.concatenate([cs[:, :D], cs[:, 2 * D :]], axis=1), 2 * r1, 2 * r1, n)
            for q in range(3):
                gT = gq[D * q : D * (q + 1), :D].T
                for k in range(n):
                    stage[k, r1 * q : r1 * (q + 1), :] = gT[r1 * k : r1 * (k + 1)]
            for k in range(n):
                stage[k, 3 * r1 : 3 * r1 + 1, :128] = sm[k : k + 1]
            emit(me, stage, keep_ref, send_ref, n, bits)


def pack_rest(pj_ref, up_ref, dn_ref, out_ref, *, n):
    r1 = D // n
    out_ref[:r1, :] = pj_ref[...]
    for q in range(4):
        out_ref[r1 * (1 + q) : r1 * (2 + q), :] = up_ref[:, D * q : D * (q + 1)]
    out_ref[5 * r1 : 9 * r1, :] = dn_ref[...]
    out_ref[9 * r1 :, :] = jnp.zeros((rest_rows(n) - 9 * r1, D), bf16)


def total_of(refs):
    total = refs[0][0]
    for got in refs[1:]:
        total = total + got[0].astype(f32)
    return total


def finish_mlp(*refs, n):
    *parts, pj, pb, gain, shift, up, ub, dn, db = refs
    r1, r4 = D // n, FF // n
    t = total_of(parts)
    pj[...] = t[:r1]
    for q in range(4):
        up[:, D * q : D * (q + 1)] = t[r1 * (1 + q) : r1 * (2 + q)]
    dn[...] = t[5 * r1 : 9 * r1]
    for i, out in enumerate((gain, shift, pb, db)):
        out[...] = t[9 * r1, r1 * i : r1 * (i + 1)]
    ub[...] = t[9 * r1, 4 * r1 : 4 * r1 + r4]


def finish_attn(*refs, n):
    *parts, gain, shift, qkv, qv = refs
    r1 = D // n
    t = total_of(parts)
    for q in range(3):
        qkv[:, D * q : D * (q + 1)] = t[r1 * q : r1 * (q + 1)]
    for i, out in enumerate((gain, shift)):
        out[...] = t[3 * r1, r1 * i : r1 * (i + 1)]
    qv[...] = t[3 * r1, 2 * r1 : 4 * r1]


def finish(body, parts, n, shapes):
    return pl.pallas_call(
        lambda *refs: body(*refs, n=n), name="finish", out_shape=[shape_of(*s) for s in shapes])(*parts)


def img(shape, at=0, count=NI):
    return pl.BlockSpec((count,) + shape, lambda i: (i + at // count,) + (0,) * len(shape))


def res(shape):
    return pl.BlockSpec(shape, lambda i: (0,) * len(shape))


smem = pl.BlockSpec(memory_space=pltpu.SMEM)
hbm = pl.BlockSpec(memory_space=pl.ANY)


def params(mib):
    return pltpu.CompilerParams(dimension_semantics=("arbitrary",), vmem_limit_bytes=mib * 2**20)


def shape_of(*dims, dtype=f32):
    return jax.ShapeDtypeStruct(dims, dtype)


def vmem(*dims, dtype=bf16):
    return pltpu.VMEM(dims, dtype)


def vec_specs(vecs):
    return [pl.BlockSpec(v.shape, lambda i: (0,)) for v in vecs]


def run_fwd(n, me, vecs, weights, x, at, count, kept=()):
    m = x.shape[0]
    lead = not kept
    shapes = [(3 * D, SL), (H, SR, SL), (D, SL)]
    out_specs = [img(s, at, NF) for s in shapes]
    out_shape = [shape_of(m, *s, dtype=bf16) for s in shapes]
    scratch = [vmem(3 * D, SL, dtype=f32), vmem(NF, SL, D)]
    if lead:
        out_specs, out_shape = out_specs + [res((3 * D, D))], out_shape + [shape_of(3 * D, D, dtype=bf16)]
        scratch = scratch + [vmem(D, 3 * D)]
    ins = [*vecs] + ([me] if lead else []) + list(weights) + [x]
    return pl.pallas_call(
        lambda *refs: attn_fwd(*refs, n=n, lead=lead), grid=(count // NF,), name="attn_fwd",
        in_specs=vec_specs(vecs) + ([smem] if lead else []) + [res(w.shape) for w in weights] + [img((S, D), at, NF)]
        + [hbm] * len(kept),
        out_specs=out_specs, out_shape=out_shape, scratch_shapes=scratch,
        input_output_aliases={len(ins) + i: i for i in range(len(kept))},
        compiler_params=params(60),
    )(*ins, *kept)


def chunk_rows(n, parts):
    return -(-(parts * (D // n) + 1) // 16) * 16


def run_mlp(n, bits, me, vecs, ga, gb, x, oT, e):
    m = x.shape[0]
    cr = chunk_rows(n, 9)
    return pl.pallas_call(
        lambda *refs: mlp(*refs, n=n, bits=bits), grid=(m // NI,), name="mlp",
        in_specs=vec_specs(vecs) + [smem, res(ga.shape), res(gb.shape), img((S, D)), img((D, SL)), img((S, D))],
        out_specs=[img((S, D)), img((S, D)), img((D, SL)), res((n // 2, cr, D)), res((n // 2, cr, D))],
        out_shape=[shape_of(m, S, D), shape_of(m, S, D), shape_of(m, D, SL, dtype=bf16),
                   shape_of(n // 2, cr, D), shape_of(n // 2, cr, D, dtype=bf16)],
        scratch_shapes=[vmem(NI, SR, D), vmem(NI, SR, D), vmem(NI, SL, D), vmem(D, D), vmem(D, FF), vmem(FF, D),
                        vmem(D + 16, FF, dtype=f32), vmem(D, FF, dtype=f32), vmem(D, D, dtype=f32),
                        vmem(8, FF, dtype=f32), vmem(n, cr, D, dtype=f32), vmem(FF, D), vmem(D, FF),
                        vmem(NI, SR, FF), vmem(NI, SR, FF), vmem(NI, D + 16, SR), vmem(1, FF, dtype=f32)],
        compiler_params=params(60),
    )(*vecs, me, ga, gb, x, oT, e)


def run_bwd(n, bits, me, vecs, x, pt, wt, doT, dx1, wT, at, count, kept=()):
    m = x.shape[0]
    cr = chunk_rows(n, 3)
    lead, last = not kept, at + count == m
    out_specs, out_shape = [img((S, D), at)], [shape_of(m, S, D)]
    scratch = [vmem(NI, SR, 512), vmem(NI, 3 * D, SR), vmem(NI, H, SR, SL)]
    sums = [(3 * D, 512), (8, 2 * D)]
    if last:
        out_specs = out_specs + [res((n // 2, cr, D))] * 2
        out_shape = out_shape + [shape_of(n // 2, cr, D), shape_of(n // 2, cr, D, dtype=bf16)]
        scratch = scratch + [vmem(*s, dtype=f32) for s in sums] + [vmem(n, cr, D, dtype=f32)]
    else:
        out_specs, out_shape = out_specs + [res(s) for s in sums], out_shape + [shape_of(*s) for s in sums]
    return pl.pallas_call(
        lambda *refs: attn_bwd(*refs, n=n, bits=bits, lead=lead, last=last), grid=(count // NI,), name="attn_bwd",
        in_specs=vec_specs(vecs)
        + [smem, img((S, D), at), img((3 * D, SL), at), img((H, SR, SL), at), img((D, SL), at), img((S, D), at), res((3 * D, D))]
        + ([] if lead else [res(s) for s in sums] + [hbm]),
        out_specs=out_specs, out_shape=out_shape, scratch_shapes=scratch,
        input_output_aliases={} if lead else {11: 0},
        compiler_params=params(60),
    )(*vecs, me, x, pt, wt, doT, dx1, wT, *kept)


def swap_mask(v, mask, n):
    return lax.ppermute(v, "dp", [(i, i ^ mask) for i in range(n)])


def swap(v, bit, n):
    return swap_mask(v, 1 << bit, n)


def pick(low, a, b):
    return jnp.where(low, jnp.concatenate([a, b], axis=0), jnp.concatenate([b, a], axis=0))


def gather_halves(v, at, n, paired):
    bits = stage_bits(n)
    low = {b: (at >> b) & 1 == 0 for b in bits}
    alone = bits[:-2] if paired else bits
    for b in alone:
        other = swap(v, b, n)
        v = pick(low[b], v, other)
    if paired:
        got = []
        for w in (1, 2, 3):
            mask = ((w & 1) << bits[-2]) | ((w >> 1) << bits[-1])
            got.append(swap_mask(v, mask, n))
        near, far = (v, got[0]), (got[1], got[2])
        b0, b1 = low[bits[-2]], low[bits[-1]]
        v = pick(b1, pick(b0, *near), pick(b0, *far))
    return v, swap(v, 0, n)


def reduce_parts(keep, send, n, bits):
    got = swap(send, 0, n)
    total = keep + got.astype(f32)
    for i in range(0, len(bits), 2):
        pair = bits[i : i + 2]
        ways = 1 << len(pair)
        size = total.shape[0] // ways
        rest = total[size:].astype(bf16)
        parts = [total[:size]]
        for w in range(1, ways):
            mask = sum(((w >> (len(pair) - 1 - j)) & 1) << b for j, b in enumerate(pair))
            parts.append(swap_mask(rest[size * (w - 1) : size * w], mask, n))
        total = parts[0]
        for got in parts[1:]:
            total = total + got.astype(f32)
    return parts


def on_device(n, block_input, first_gain, first_shift, qkv_weight, query_value_bias, proj_weight, proj_bias,
              second_gain, second_shift, up_weight, up_bias, down_weight, down_bias, output_cotangent):
    n_bits = n.bit_length() - 1
    bits = tuple(range(1, n_bits))
    r1, r4 = D // n, FF // n
    at = lax.axis_index("dp").astype(jnp.int32)
    me = at.reshape(1)

    qa, qb = gather_halves(qkv_weight, at, n, False)
    rest = pl.pallas_call(
        lambda *refs: pack_rest(*refs, n=n), name="pack",
        out_shape=shape_of(rest_rows(n), D, dtype=bf16))(proj_weight, up_weight, down_weight)
    wa, wb = gather_halves(rest, at, n, True)
    m = block_input.shape[0]
    acts, wT = (), None
    vecs = (first_gain, first_shift, query_value_bias)
    for i, (lo, hi) in enumerate(zip((0,) + FWD_CUTS, FWD_CUTS + (m,))):
        made = run_fwd(n, me, vecs, (qa, qb) if i == 0 else (wT,), block_input, lo, hi - lo, acts)
        acts, wT = made[:3], made[3] if i == 0 else wT
    pt, wt, oT = acts
    vecs = (proj_bias, second_gain, second_shift, up_bias, down_bias)
    out, dx1, doT, keep, send = run_mlp(n, bits, me, vecs, wa, wb, block_input, oT, output_cotangent)
    mp = reduce_parts(keep, send, n, bits)
    kept = ()
    vecs = (first_gain, first_shift)
    for lo, hi in zip((0,) + BWD_CUTS, BWD_CUTS + (m,)):
        made = run_bwd(n, bits, me, vecs, block_input, pt, wt, doT, dx1, wT, lo, hi - lo, kept)
        kept = (made[1], made[2], made[0])
    din, keep, send = made
    ap = reduce_parts(keep, send, n, bits)
    g_proj, g_pb, gain2, shift2, g_up, g_ub, g_down, g_db = finish(
        finish_mlp, mp, n, [(r1, D), (r1,), (r1,), (r1,), (r1, FF), (r4,), (r4, D), (r1,)])
    gain1, shift1, g_qkv, g_qv = finish(finish_attn, ap, n, [(r1,), (r1,), (r1, 3 * D), (2 * r1,)])
    return (out, din, gain1, shift1, g_qkv, g_qv, g_proj, g_pb, gain2, shift2, g_up, g_ub, g_down, g_db)


def solution(mesh):
    rows, vec, imgs = P("dp", None), P("dp"), P("dp", None, None)
    n = mesh.shape["dp"]

    def body(*args):
        return on_device(n, *args)

    return jax.shard_map(
        body, mesh=mesh,
        in_specs=(imgs, P(), P(), rows, P(), rows, P(), P(), P(), rows, P(), rows, P(), imgs),
        out_specs=(imgs, imgs, vec, vec, rows, vec, rows, vec, vec, vec, rows, vec, rows, vec),
        check_vma=False)
```
